128 devices in a mesh: row: 8 (over x, y_hi), col: 16 (over y_lo, z, core).
Axes of the slice: x: 4, y: 4 (y_hi: 2, y_lo: 2; y = y_hi * 2 + y_lo), z: 4, core: 2. Of those that a mesh axis runs over, the one named last changes fastest.
Arguments:
- ancestor: float32 [24576, 24576], P('row', 'col'), may hold values from -6 to 6
- panels: float32 [4, 16, 256, 512], P(None, 'col'), may hold values from -0.09375 to 0.09375
- diag_inverse: float32 [4, 512, 512], P(None, 'row'), may hold values from -6 to 6
- fill_strips: int32 [4, 16], replicated, may hold values from 0 to 95, as said below
Outputs:
- upper_strips: float32 [4, 16, 256, 512], P(None, 'col')
- diagonal_blocks: float32 [4, 512, 512], P(None, 'row')
The draws below stay inside these ranges and needn't reach their ends.
Inputs may be any that keep to these rules, and one draw needn't show every extreme that they name: `fill_strips`: each row lists 16 different strips in no particular order; of the strips s with the same s // 6 a row lists at most 2, and exactly 2 for some value; of the strips with the same s // 12 it lists at most 4, and exactly that many for some value.
All inputs are finite; a program needn't handle non-finite values.
Results may differ from the reference program's by a relative error of at most 0.0001.
Values sent between devices are 32-bit elements; how exact they have to be, the bound alone decides.
No kernel may reach another device: no remote copies, remote signals or barrier semaphores. Data moves between devices by JAX's collectives and lax.ppermute only.
A program may use at most 192 MiB of HBM per device.

```python
import jax
import jax.numpy as jnp
from jax import lax

M = 24576
W = 512
STRIP = 256
NSUP = 4
FILL_DEV = 1
FILL = 16
STRIPS = 96
N_ROW = 8


def draw_fill_strips(key, part):
    columns = FILL // FILL_DEV
    per_col = STRIPS // columns
    per_row = columns // N_ROW
    listing = []
    for supernode in range(NSUP):
        base = jax.random.fold_in(key, 211 + supernode)
        busy = jax.random.randint(jax.random.fold_in(base, 1), (), 0, N_ROW, dtype=jnp.int32)
        ids = jnp.arange(columns, dtype=jnp.int32)
        in_busy = (ids // per_row == busy).astype(jnp.int32)
        scores = jax.random.randint(jax.random.fold_in(base, 2), (columns,), 0, 65536, dtype=jnp.int32) * columns + ids
        scores = scores * (1 - in_busy) - in_busy
        emptied = lax.top_k(scores, per_row)[1].astype(jnp.int32)
        empty_mask = jnp.sum((ids[:, None] == emptied[None, :]).astype(jnp.int32), axis=1)
        counts = 1 + in_busy - empty_mask
        picks = jax.random.randint(jax.random.fold_in(base, 3), (columns, per_col), 0, 65536, dtype=jnp.int32) * per_col + jnp.arange(per_col, dtype=jnp.int32)[None, :]
        chosen = lax.top_k(picks, 2)[1].astype(jnp.int32)
        lower = jnp.min(chosen, axis=1)
        upper = jnp.max(chosen, axis=1)
        strips = jnp.stack([ids * per_col + lower, ids * per_col + upper], axis=1).reshape(-1)
        valid = jnp.stack([counts >= 1, counts >= 2], axis=1).reshape(-1).astype(jnp.int32)
        order = jnp.argsort((1 - valid) * (2 * columns) + jnp.arange(2 * columns, dtype=jnp.int32))
        sorted_strips = strips[order[:FILL]]
        before = jnp.cumsum(counts) - counts - ids
        good = jnp.logical_and(before <= 0, before + counts >= 1).astype(jnp.int32)
        anchor = jnp.argmax(good).astype(jnp.int32)
        shuffle = jax.random.permutation(jax.random.fold_in(base, 4), FILL).astype(jnp.int32)
        where_anchor = jnp.argmax((shuffle == anchor).astype(jnp.int32)).astype(jnp.int32)
        target = (anchor + FILL // 2) % FILL
        shuffle = jnp.where(ids == target, anchor, jnp.where(ids == where_anchor, shuffle[target], shuffle))
        listing.append(sorted_strips[shuffle])
    return jnp.stack(listing).astype(jnp.int32)


def steps_of(stream_key, dims, cuts, low, largest):
    loudness = 1.0
    for dim, blocks in cuts:
        steps = jax.random.uniform(jax.random.fold_in(jax.random.fold_in(stream_key, 6), dim), (blocks,), jnp.float32, low / len(cuts), largest / len(cuts))
        loudness = loudness * jnp.repeat(jnp.exp(steps), dims[dim] // blocks).reshape((-1,) + (1,) * (len(dims) - 1 - dim))
    return loudness


def gaussian(own_key, extent, scale, bound, pieces=(), kind=jnp.bfloat16):
    entries = scale * jax.random.normal(own_key, extent, jnp.float32)
    if pieces:
        entries = entries * steps_of(own_key, extent, pieces, -0.22, 0.18)
    return jnp.clip(entries, -bound, bound).astype(kind)


def setup_inputs(seed: int = 0) -> dict:
    arg_keys = jax.random.split(jax.random.key(seed), 5)
    return {
        "ancestor": gaussian(arg_keys[0], (M, M), 1.0, 6.0, ((0, 8), (1, 16)), jnp.float32),
        "panels": gaussian(arg_keys[1], (NSUP, FILL, STRIP, W), (FILL * STRIP) ** -0.5, 0.09375, ((1, 16),), jnp.float32),
        "diag_inverse": gaussian(arg_keys[2], (NSUP, W, W), 1.0, 6.0, ((1, 8),), jnp.float32),
        "fill_strips": draw_fill_strips(jax.random.fold_in(arg_keys[4], 71), 0),
    }


def reference(ancestor, panels, diag_inverse, fill_strips):
    offsets = jnp.arange(STRIP, dtype=jnp.int32)
    uppers = []
    diagonals = []
    for supernode in range(NSUP):
        row_ids = (fill_strips[supernode][:, None].astype(jnp.int32) * STRIP + offsets[None, :]).reshape(-1).astype(jnp.int32)
        selected = jnp.take(jnp.take(ancestor, row_ids, axis=0), row_ids, axis=1)
        factor = panels[supernode].reshape(FILL * STRIP, W)
        upper = -jnp.dot(selected, factor, precision=lax.Precision.HIGHEST, preferred_element_type=jnp.float32)
        diagonal = diag_inverse[supernode] - jnp.dot(factor.T, upper, precision=lax.Precision.HIGHEST, preferred_element_type=jnp.float32)
        uppers.append(upper.reshape(FILL, STRIP, W))
        diagonals.append(diagonal)
    return jnp.stack(uppers), jnp.stack(diagonals)
```

```python
import functools

import jax
import jax.numpy as jnp
from jax import lax
from jax.experimental import pallas as pl
from jax.experimental.pallas import tpu as pltpu
from jax.sharding import Mesh
from jax.sharding import PartitionSpec as P


AXES = ("x", "h", "l", "z", "c")
SIZES = (4, 2, 2, 4, 2)
ROW, COL, PLANE = ("x", "h"), ("l", "z", "c"), ("l", "z")
S = 256
W = 512
K = 4
F = 16
HALF = W // 2
PIECE = S // 8
LANES = 128
STEPS = (0, 3, 1, 2)
LIMIT = 60 * 1024 * 1024


def col_of(strip):
    return (strip * 43) >> 8


def row_of(strip):
    return col_of(strip) >> 1


def split(value):
    high = value.astype(jnp.bfloat16)
    low = (value - high.astype(jnp.float32)).astype(jnp.bfloat16)
    return high, low


def dot3(left, right, dims):
    (lh, ll), (rh, rl) = left, right
    one = functools.partial(
        lax.dot_general, dimension_numbers=(dims, ((), ())), preferred_element_type=jnp.float32
    )
    return one(lh, rh) + (one(lh, rl) + one(ll, rh))


def halves_kernel(info, fs, panel, keep, send):
    c = info[3]
    own = pl.multiple_of(c * HALF, HALF)
    other = pl.multiple_of((1 - c) * HALF, HALF)
    keep[...] = panel[0, 0, :, pl.ds(own, HALF)].reshape(8, PIECE, HALF)
    send[...] = panel[0, 0, :, pl.ds(other, HALF)].reshape(8, PIECE, HALF)


def gather_kernel(info, fs, ancestor, out, rows, cols, sems):
    r = info[0] * 2 + info[1]
    col = info[2] * 2 + info[3]
    copies = []
    for k in range(K):
        for i in range(8):
            rows[k * 8 + i] = r * 12
        for i in range(4):
            cols[k * 4 + i] = col * 6
        nr = jnp.int32(0)
        nc = jnp.int32(0)
        for p in range(F):
            strip = fs[k * F + p]
            rows[k * 8 + jnp.minimum(nr, 7)] = strip
            cols[k * 4 + jnp.minimum(nc, 3)] = strip
            nr = nr + (row_of(strip) == r).astype(jnp.int32)
            nc = nc + (col_of(strip) == col).astype(jnp.int32)
        for i in range(4):
            low = pl.multiple_of(jnp.clip(rows[k * 8 + i] - r * 12, 0, 11) * S, S)
            for j in range(2):
                left = pl.multiple_of(jnp.clip(cols[k * 4 + j] - col * 6, 0, 5) * S, S)
                copy = pltpu.make_async_copy(
                    ancestor.at[pl.ds(low, S), pl.ds(left, S)],
                    out.at[k, i, :, pl.ds(j * S, S)],
                    sems.at[k, i, j],
                )
                copy.start()
                copies.append(copy)
    for copy in copies:
        copy.wait()


def route_kernel(info, fs, pieces, out, table, count):
    x, c = info[0], info[3]
    for i in range(2 * F):
        table[i] = 0
    for i in range(F):
        count[i] = 0
    for p in range(F):
        col = col_of(fs[x * F + p])
        n = count[col]
        table[col * 2 + jnp.minimum(n, 1)] = p
        count[col] = n + 1
    for i in range(2 * F):
        out[i] = pieces[table[i] ^ c]


def product_kernel(steps, info, fs, *refs):
    out = refs[-1]
    refs = list(refs[:-1])
    x, c = info[0], info[3]
    r = x * 2 + info[1]
    col = info[2] * 2 + c
    out[...] = jnp.zeros_like(out)
    for n, step in enumerate(steps):
        parts = 2 if step == 2 else 1
        mine, theirs = refs.pop(0), refs.pop(0)
        panels = [refs.pop(0) for _ in range(parts)]
        k = (x + step) & 3
        nr = jnp.int32(0)
        nc = [jnp.int32(0), jnp.int32(0)]
        for p in range(F):
            strip = fs[k * F + p]
            nr = nr + (row_of(strip) == r).astype(jnp.int32)
            for side in range(2):
                nc[side] = nc[side] + (col_of(strip) == (col ^ side)).astype(jnp.int32)
        for side, tiles in enumerate((mine, theirs)):
            for j in range(2):

                @pl.when(j < nc[side])
                def _():
                    slot = (c ^ side) * 2 + j
                    pieces = [ref[:, slot] for ref in panels]
                    whole = pieces[0] if parts == 1 else jnp.concatenate(pieces, axis=0)
                    right = split(whole.reshape(S, HALF))

                    def body(i, carry):
                        left = split(tiles[0, i, :, j * S : (j + 1) * S])
                        value = dot3(left, right, ((1,), (0,)))
                        out[:, n, i] += value.reshape(8, PIECE, HALF)
                        return carry

                    lax.fori_loop(0, jnp.minimum(nr, 4), body, 0)


def sums_kernel(info, fs, first, middle, last, out):
    x = info[0]
    for n, step in enumerate(STEPS):
        k = (x + step) & 3
        if n == 0:
            parts = [first[q, 0] for q in range(8)]
        elif n == 3:
            parts = [last[q, 0] for q in range(8)]
        else:
            parts = [middle[q, n - 1] for q in range(8)]
        total = parts[0]
        for part in parts[1:]:
            total = total + part
        out[k * 2] = total[:, :, :LANES]
        out[k * 2 + 1] = total[:, :, LANES:]


def homes_kernel(info, fs, pieces, out, count):
    x, c = info[0], info[3]
    for i in range(8):
        count[i] = 0
    for p in range(F):
        r = row_of(fs[x * F + p])
        n = count[r]
        count[r] = n + 1
        out[p ^ c] = pieces[r * 4 + jnp.minimum(n, 3)]


def assemble_kernel(info, fs, own, other, across, out):
    h, c = info[1], info[3]
    for value, ch, hh in (
        (own[...], c, h),
        (other[...], 1 - c, h),
        (across[0], c, 1 - h),
        (across[1], 1 - c, 1 - h),
    ):
        lane = pl.multiple_of(ch * HALF + hh * LANES, LANES)
        out[:, pl.ds(lane, LANES)] = value.reshape(S, LANES)


def finish_kernel(info, fs, panels, own, before, after, top, bottom, upper, keep, send, tmp):
    x, h, c = info[0], info[1], info[3]
    r = x * 2 + h
    lanes = pl.multiple_of((r >> 1) * LANES, LANES)
    low = pl.multiple_of((r & 1) * 64, 64)
    for n, step in enumerate(STEPS):
        k = (x + step) & 3
        if n == 3:
            value = jnp.concatenate([top[...], bottom[...]], axis=0)
        else:
            value = (own, before, after)[n][...]
        upper[k, 0] = -value
        left = split(panels[k, 0, :, pl.ds(lanes, LANES)])
        tmp[...] = dot3(left, split(value), ((0,), (0,)))
        keep[k] = tmp[pl.ds(low, 64), pl.ds(pl.multiple_of(c * HALF, HALF), HALF)]
        send[k] = tmp[pl.ds(low, 64), pl.ds(pl.multiple_of((1 - c) * HALF, HALF), HALF)]


VMEM = pl.BlockSpec(memory_space=pltpu.VMEM)


def call(kernel, name, info, fs, args, out_shapes, in_specs=None, scratch=(), flops=0):
    single = not isinstance(out_shapes, list)
    shapes = [out_shapes] if single else out_shapes
    out_shape = [jax.ShapeDtypeStruct(s, jnp.float32) for s in shapes]
    moved = 4 * sum(functools.reduce(lambda a, b: a * b, s) for s in shapes)
    result = pl.pallas_call(
        kernel,
        out_shape=out_shape[0] if single else out_shape,
        grid_spec=pltpu.PrefetchScalarGridSpec(
            num_scalar_prefetch=2,
            grid=(1,),
            in_specs=in_specs or [VMEM] * len(args),
            out_specs=VMEM if single else [VMEM] * len(shapes),
            scratch_shapes=list(scratch),
        ),
        compiler_params=pltpu.CompilerParams(vmem_limit_bytes=LIMIT),
        cost_estimate=pl.CostEstimate(flops=flops, bytes_accessed=2 * moved, transcendentals=0),
        name=name,
    )(info, fs, *args)
    return result


def hop(value, axis, shift):
    size = SIZES[AXES.index(axis)]
    return lax.ppermute(value, axis, [(i, (i + shift) % size) for i in range(size)])


def exchange(value, axes):
    return lax.all_to_all(value, axes, 0, 0, tiled=True)


def gather_x(value):
    half = value.shape[0] // 2
    before = hop(value, "x", 1)
    after = hop(value, "x", -1)
    top = hop(before[:half], "x", 1)
    bottom = hop(after[half:], "x", -1)
    return before, after, top, bottom


def local(ancestor, panels, diag_inverse, fill_strips):
    x, h, c = lax.axis_index("x"), lax.axis_index("h"), lax.axis_index("c")
    q = lax.axis_index(PLANE)
    info = jnp.stack([x, h, q, c]).astype(jnp.int32)
    fs = fill_strips.reshape(-1)

    keep, send = call(
        halves_kernel, "halves", info, fs, [panels], [(8, PIECE, HALF)] * 2,
        in_specs=[pl.BlockSpec((1, 1, S, W), lambda i, info, fs: (info[0], 0, 0, 0))],
    )
    got = hop(send, "c", 1)
    tiles = call(
        gather_kernel, "gather", info, fs, [ancestor], (K, 4, S, 2 * S),
        in_specs=[pl.BlockSpec(memory_space=pl.ANY)],
        scratch=[pltpu.SMEM((K * 8,), jnp.int32), pltpu.SMEM((K * 4,), jnp.int32),
                 pltpu.SemaphoreType.DMA((K, 4, 2))],
    )
    their_tiles = hop(tiles, "c", 1)
    pieces = exchange(jnp.stack([keep, got], axis=1), PLANE)
    routed = call(
        route_kernel, "route", info, fs, [pieces.reshape(F, PIECE, HALF)], (2 * F, PIECE, HALF),
        scratch=[pltpu.SMEM((2 * F,), jnp.int32), pltpu.SMEM((F,), jnp.int32)],
    )
    panel = exchange(routed.reshape(8, 4, PIECE, HALF), PLANE)
    before, after, top, bottom = gather_x(panel)

    def tile_spec(step):
        return pl.BlockSpec(
            (1, 4, S, 2 * S), lambda i, info, fs: ((info[0] + step) & 3, 0, 0, 0)
        )

    def product(steps, blocks, name):
        args, specs = [], []
        for step, block in zip(steps, blocks, strict=True):
            args += [tiles, their_tiles, *block]
            specs += [tile_spec(step)] * 2 + [VMEM] * len(block)
        out = call(
            functools.partial(product_kernel, steps), name, info, fs, args,
            (8, len(steps), 4, PIECE, HALF), in_specs=specs, flops=len(steps) * 10**9,
        )
        return exchange(out, PLANE)

    first = product((0,), [[panel]], "product_own")
    middle = product((3, 1), [[before], [after]], "product_near")
    last = product((2,), [[top, bottom]], "product_far")
    sums = call(sums_kernel, "sums", info, fs, [first, middle, last], (8, 4, PIECE, LANES))
    by_row = exchange(sums, ROW)
    homes = call(
        homes_kernel, "homes", info, fs, [by_row.reshape(32, PIECE, LANES)], (F, PIECE, LANES),
        scratch=[pltpu.SMEM((8,), jnp.int32)],
    )
    placed = exchange(homes.reshape(8, 2, PIECE, LANES), PLANE)
    own = placed[:, 0]
    other = hop(placed[:, 1], "c", 1)
    across = hop(jnp.stack([own, other]), "h", 1)
    strip = call(assemble_kernel, "assemble", info, fs, [own, other, across], (S, W))
    upper, part, part_send = call(
        finish_kernel, "finish", info, fs, [panels, strip, *gather_x(strip)],
        [(K, 1, S, W), (K, 64, HALF), (K, 64, HALF)],
        scratch=[pltpu.VMEM((LANES, W), jnp.float32)],
    )
    part = (part + hop(part_send, "c", 1)).reshape(8, PIECE, HALF)
    part = exchange(part, PLANE).sum(0)
    part = exchange(jnp.broadcast_to(part[None], (8, PIECE, HALF)), PLANE).reshape(K, 64, HALF)
    theirs = hop(part, "c", 1)
    total = jnp.where(
        c == 0,
        jnp.concatenate([part, theirs], axis=2),
        jnp.concatenate([theirs, part], axis=2),
    )
    return upper, diag_inverse + total


def solution(mesh):
    return jax.shard_map(
        local,
        mesh=Mesh(mesh.devices.reshape(SIZES), AXES),
        in_specs=(P(ROW, COL), P(None, COL, None, None), P(None, ROW, None), P()),
        out_specs=(P(None, COL, None, None), P(None, ROW, None)),
        check_vma=False,
    )
```

```python
import functools

import jax
import jax.numpy as jnp
from jax import lax
from jax.experimental import pallas as pl
from jax.experimental.pallas import tpu as pltpu
from jax.sharding import Mesh
from jax.sharding import PartitionSpec as P


AXES = ("x", "h", "l", "z", "c")
SIZES = (4, 2, 2, 4, 2)
ROW, COL, PLANE = ("x", "h"), ("l", "z", "c"), ("l", "z")
S = 256
W = 512
K = 4
F = 16
HALF = W // 2
PIECE = S // 8
LANES = 128
STEPS = (0, 3, 1, 2)
LIMIT = 60 * 1024 * 1024


def col_of(strip):
    return (strip * 43) >> 8


def row_of(strip):
    return col_of(strip) >> 1


def split(value):
    high = value.astype(jnp.bfloat16)
    low = (value - high.astype(jnp.float32)).astype(jnp.bfloat16)
    return high, low


def dot3(left, right, dims):
    (lh, ll), (rh, rl) = left, right
    one = functools.partial(
        lax.dot_general, dimension_numbers=(dims, ((), ())), preferred_element_type=jnp.float32
    )
    return one(lh, rh) + (one(lh, rl) + one(ll, rh))


def pack_kernel(info, fs, panel, out):
    for ch in range(2):
        out[:, ch] = panel[0, 0, :, ch * HALF : (ch + 1) * HALF].reshape(8, PIECE, HALF)


def count_if(fs, k, test):
    total = jnp.int32(0)
    for p in range(F):
        total = total + test(fs[k, p]).astype(jnp.int32)
    return total


def gather_kernel(info, fs, ancestor, after, out, tiles, rows, cols, sems, out_sems):
    r = info[0] * 2 + info[1]
    col = info[2] * 2 + info[3]
    moves = []
    for k in range(K):
        nr = jnp.int32(0)
        nc = jnp.int32(0)
        for i in range(8):
            rows[k * 8 + i] = r * 12
        for i in range(4):
            cols[k * 4 + i] = col * 6
        for p in range(F):
            strip = fs[k, p]
            rows[k * 8 + jnp.minimum(nr, 7)] = strip
            cols[k * 4 + jnp.minimum(nc, 3)] = strip
            nr = nr + (row_of(strip) == r).astype(jnp.int32)
            nc = nc + (col_of(strip) == col).astype(jnp.int32)
        for i in range(4):
            low = pl.multiple_of(jnp.clip(rows[k * 8 + i] - r * 12, 0, 11) * S, S)
            for j in range(2):
                left = pl.multiple_of(jnp.clip(cols[k * 4 + j] - col * 6, 0, 5) * S, S)
                valid = jnp.logical_and(i < nr, j < nc)
                source = ancestor.at[pl.ds(low, S), pl.ds(left, S)]
                inward = pltpu.make_async_copy(source, tiles.at[k, i, j], sems.at[k, i, j])
                outward = pltpu.make_async_copy(
                    tiles.at[k, i, j], out.at[k, j, i], out_sems.at[k, i, j]
                )
                pl.when(valid)(inward.start)
                moves.append((valid, inward, outward))
    for valid, inward, outward in moves:

        @pl.when(valid)
        def _():
            inward.wait()
            outward.start()

    for valid, inward, outward in moves:
        pl.when(valid)(outward.wait)


def route_kernel(info, fs, pieces, out, table, count):
    x = info[0]
    for i in range(2 * F):
        table[i] = 0
    for i in range(F):
        count[i] = 0
    for p in range(F):
        col = col_of(fs[x, p])
        n = count[col]
        table[col * 2 + jnp.minimum(n, 1)] = p
        count[col] = n + 1
    for i in range(2 * F):
        out[i] = pieces[table[i]]


def product_kernel(steps, info, fs, mine, theirs, *refs):
    out, tiles, sems = refs[-3:]
    refs = list(refs[:-3])
    x, c = info[0], info[3]
    r = x * 2 + info[1]
    col = info[2] * 2 + c
    jobs = []
    for n, step in enumerate(steps):
        k = (x + step) & 3
        nr = jnp.minimum(count_if(fs, k, lambda strip: row_of(strip) == r), 4)
        for side, source in enumerate((mine, theirs)):
            nc = count_if(fs, k, lambda strip: col_of(strip) == (col ^ side))
            for j in range(2):
                spot = (n, side, j)
                loop = jnp.where(j < nc, nr, 0)

                def copy(i, k=k, j=j, source=source, spot=spot):
                    return pltpu.make_async_copy(
                        source.at[k, j, i], tiles.at[(*spot, i)], sems.at[(*spot, i)]
                    )

                def start(i, carry, copy=copy):
                    copy(i).start()
                    return carry

                lax.fori_loop(0, loop, start, 0)
                jobs.append((n, (c ^ side) * 2 + j, spot, loop, copy))
    out[...] = jnp.zeros_like(out)
    panels = []
    for step in steps:
        panels.append([refs.pop(0) for _ in range(2 if step == 2 else 1)])
    for n, slot, spot, loop, copy in jobs:

        @pl.when(loop > 0)
        def _():
            right = split(
                jnp.concatenate([ref[:, slot] for ref in panels[n]], axis=0).reshape(S, HALF)
            )

            def body(i, carry):
                copy(i).wait()
                value = dot3(split(tiles[(*spot, i)]), right, ((1,), (0,)))
                out[:, n, i] += value.reshape(8, PIECE, HALF)
                return carry

            lax.fori_loop(0, loop, body, 0)


def homes_kernel(info, fs, *refs):
    pieces, out, table, count = refs[:8], refs[8], refs[9], refs[10]
    x, h = info[0], info[1]
    for i in range(8):
        count[i] = 0
    for p in range(F):
        r = row_of(fs[x, p])
        n = count[r]
        table[r * 4 + jnp.minimum(n, 3)] = p
        count[r] = n + 1
    for dx in range(4):
        for dh in range(2):
            r = ((x + dx) & 3) * 2 + (h ^ dh)
            for i in range(4):

                @pl.when(i < count[r])
                def _():
                    out[table[r * 4 + i]] = pieces[dx * 2 + dh][i]


def strip_kernel(info, fs, pieces, panel, upper, keep, send, tmp):
    h, c = info[1], info[3]
    parts = [pieces[:, ch].reshape(S, HALF) for ch in range(2)]
    value = jnp.concatenate(parts, axis=1)
    upper[...] = -value
    tmp[...] = dot3(split(panel[0, 0]), split(value), ((0,), (0,)))
    for xx in range(4):
        low = pl.multiple_of((xx * 2 + h) * 64, 64)
        for out, ch in ((keep, c), (send, 1 - c)):
            lanes = pl.multiple_of(ch * HALF, HALF)
            out[:, xx] = tmp[pl.ds(low, 64), pl.ds(lanes, HALF)].reshape(8, 8, HALF)


def place_kernel(info, fs, *refs):
    upper = refs[-1]
    for ref, step in zip(refs, STEPS, strict=False):
        upper[(info[0] + step) & 3, 0] = ref[...]


def diagonal_kernel(info, fs, given, mine, theirs, out):
    c = info[3]
    for value, ch in ((mine, c), (theirs, 1 - c)):
        lanes = pl.multiple_of(ch * HALF, HALF)
        for k in range(K):
            part = value[:, k].reshape(64, HALF)
            out[k, :, pl.ds(lanes, HALF)] = given[k, :, pl.ds(lanes, HALF)] + part


VMEM = pl.BlockSpec(memory_space=pltpu.VMEM)
ANY = pl.BlockSpec(memory_space=pl.ANY)


def call(kernel, name, info, fs, args, out_shapes, in_specs=None, out_specs=None, scratch=(), flops=0):
    single = not isinstance(out_shapes, list)
    shapes = [out_shapes] if single else out_shapes
    out_shape = [jax.ShapeDtypeStruct(s, jnp.float32) for s in shapes]
    moved = 4 * sum(functools.reduce(lambda a, b: a * b, s) for s in shapes)
    result = pl.pallas_call(
        kernel,
        out_shape=out_shape[0] if single else out_shape,
        grid_spec=pltpu.PrefetchScalarGridSpec(
            num_scalar_prefetch=2,
            grid=(1,),
            in_specs=in_specs or [VMEM] * len(args),
            out_specs=out_specs or (VMEM if single else [VMEM] * len(shapes)),
            scratch_shapes=list(scratch),
        ),
        compiler_params=pltpu.CompilerParams(vmem_limit_bytes=LIMIT),
        cost_estimate=pl.CostEstimate(flops=flops, bytes_accessed=2 * moved, transcendentals=0),
        name=name,
    )(info, fs, *args)
    return result


def hop(value, axis, shift):
    size = SIZES[AXES.index(axis)]
    return lax.ppermute(value, axis, [(i, (i + shift) % size) for i in range(size)])


def exchange(value, axes):
    return lax.all_to_all(value, axes, 0, 0, tiled=True)


def row_hop(value, dx, dh):
    pairs = [(x * 2 + h, (x + dx) % 4 * 2 + (h ^ dh)) for x in range(4) for h in range(2)]
    return lax.ppermute(value, ROW, pairs)


def gather_x(value):
    half = value.shape[0] // 2
    before = hop(value, "x", 1)
    after = hop(value, "x", -1)
    top = hop(before[:half], "x", 1)
    bottom = hop(after[half:], "x", -1)
    return before, after, top, bottom


def local(ancestor, panels, diag_inverse, fs):
    x, h, c = lax.axis_index("x"), lax.axis_index("h"), lax.axis_index("c")
    info = jnp.stack([x, h, lax.axis_index(PLANE), c]).astype(jnp.int32)
    own_panel = pl.BlockSpec((1, 1, S, W), lambda i, info, fs: (info[0], 0, 0, 0))

    packed = call(
        pack_kernel, "pack", info, fs, [panels], (8, 2, PIECE, HALF), in_specs=[own_panel]
    )
    pieces = exchange(packed.reshape(F, PIECE, HALF), COL)
    tiles = call(
        gather_kernel, "gather", info, fs, [ancestor, packed], (K, 2, 4, S, S),
        in_specs=[ANY, ANY], out_specs=ANY,
        scratch=[pltpu.VMEM((K, 4, 2, S, S), jnp.float32),
                 pltpu.SMEM((K * 8,), jnp.int32), pltpu.SMEM((K * 4,), jnp.int32),
                 pltpu.SemaphoreType.DMA((K, 4, 2)), pltpu.SemaphoreType.DMA((K, 4, 2))],
    )
    their_tiles = hop(tiles, "c", 1)
    routed = call(
        route_kernel, "route", info, fs, [pieces], (2 * F, PIECE, HALF),
        scratch=[pltpu.SMEM((2 * F,), jnp.int32), pltpu.SMEM((F,), jnp.int32)],
    )
    panel = exchange(routed.reshape(8, 4, PIECE, HALF), PLANE)
    before, after, top, bottom = gather_x(panel)

    def product(steps, blocks, name, behind=()):
        args = [tiles, their_tiles, *blocks, *behind]
        n = len(steps)
        return call(
            functools.partial(product_kernel, steps), name, info, fs, args,
            (8, n, 4, PIECE, HALF), in_specs=[ANY] * 2 + [VMEM] * len(blocks) + [ANY] * len(behind),
            scratch=[pltpu.VMEM((n, 2, 2, 4, S, S), jnp.float32),
                     pltpu.SemaphoreType.DMA((n, 2, 2, 4))],
            flops=n * 10**9,
        )

    def total(value):
        return exchange(value, PLANE).sum(0)

    own_product = product((0,), [panel], "product_own")
    own = total(own_product)[0]
    near_product = product((3, 1), [before, after], "product_near", [own])
    near = total(near_product)
    far_product = product((2,), [top, bottom], "product_far", [near_product])
    near, far_product = lax.optimization_barrier((near, far_product))
    far = total(far_product)[0]
    sources = [
        own, row_hop(own, 0, 1),
        row_hop(near[0], -1, 0), row_hop(near[0], -1, 1),
        row_hop(far, 2, 0), row_hop(far, 2, 1),
        row_hop(near[1], 1, 0), row_hop(near[1], 1, 1),
    ]
    homes = call(
        homes_kernel, "homes", info, fs, sources, (F, PIECE, HALF),
        scratch=[pltpu.SMEM((32,), jnp.int32), pltpu.SMEM((8,), jnp.int32)],
    )
    placed = exchange(homes, COL).reshape(8, 2, PIECE, HALF)
    strip, part, part_send = call(
        strip_kernel, "strip", info, fs, [placed, panels],
        [(S, W), (8, 4, 8, HALF), (8, 4, 8, HALF)], in_specs=[VMEM, own_panel],
        scratch=[pltpu.VMEM((W, W), jnp.float32)],
    )
    part = total(part + hop(part_send, "c", 1))
    strips = [strip, hop(strip, "x", 1), hop(strip, "x", -1), hop(strip, "x", 2)]
    upper = call(place_kernel, "place", info, fs, strips, (K, 1, S, W))
    part = exchange(part, ("x",))
    part = exchange(jnp.broadcast_to(part[None], (8, *part.shape)), PLANE)
    diagonal = call(
        diagonal_kernel, "diagonal", info, fs, [diag_inverse, part, hop(part, "c", 1)], (K, 64, W)
    )
    return upper, diagonal


def solution(mesh):
    return jax.shard_map(
        local,
        mesh=Mesh(mesh.devices.reshape(SIZES), AXES),
        in_specs=(P(ROW, COL), P(None, COL, None, None), P(None, ROW, None), P()),
        out_specs=(P(None, COL, None, None), P(None, ROW, None)),
        check_vma=False,
    )
```

```python
import functools

import jax
import jax.numpy as jnp
from jax import lax
from jax.experimental import pallas as pl
from jax.experimental.pallas import tpu as pltpu
from jax.sharding import Mesh
from jax.sharding import PartitionSpec as P


AXES = ("x", "h", "l", "z", "c")
SIZES = (4, 2, 2, 4, 2)
ROW, COL, PLANE = ("x", "h"), ("l", "z", "c"), ("l", "z")
SHEET = ("h", *PLANE)
S = 256
W = 512
K = 4
F = 16
HALF = W // 2
FRONT = S // 8
PIECE = S // 16
STEPS = (0, 3, 1, 2)
LIMIT = 60 * 1024 * 1024


def col_of(strip):
    return (strip * 43) >> 8


def row_of(strip):
    return col_of(strip) >> 1


def split(value):
    high = value.astype(jnp.bfloat16)
    low = (value - high.astype(jnp.float32)).astype(jnp.bfloat16)
    return high, low


def dot3(left, right, dims):
    (lh, ll), (rh, rl) = left, right
    one = functools.partial(
        lax.dot_general, dimension_numbers=(dims, ((), ())), preferred_element_type=jnp.float32
    )
    return one(lh, rh) + (one(lh, rl) + one(ll, rh))


def pack_kernel(info, fs, panel, out):
    for ch in range(2):
        out[:, ch] = panel[0, 0, :, ch * HALF : (ch + 1) * HALF].reshape(8, FRONT, HALF)


def count_if(fs, k, test):
    total = jnp.int32(0)
    for p in range(F):
        total = total + test(fs[k, p]).astype(jnp.int32)
    return total


def gather_kernel(info, fs, ancestor, after, first, rest, tiles, rows, cols, sems, out_sems):
    r = info[0] * 2 + info[1]
    col = info[2] * 2 + info[3]
    moves = []
    for n, step in enumerate(STEPS):
        k = (info[0] + step) & 3
        nr = jnp.int32(0)
        nc = jnp.int32(0)
        for i in range(8):
            rows[n * 8 + i] = r * 12
        for i in range(4):
            cols[n * 4 + i] = col * 6
        for p in range(F):
            strip = fs[k, p]
            rows[n * 8 + jnp.minimum(nr, 7)] = strip
            cols[n * 4 + jnp.minimum(nc, 3)] = strip
            nr = nr + (row_of(strip) == r).astype(jnp.int32)
            nc = nc + (col_of(strip) == col).astype(jnp.int32)
        for i in range(4):
            low = pl.multiple_of(jnp.clip(rows[n * 8 + i] - r * 12, 0, 11) * S, S)
            for j in range(2):
                left = pl.multiple_of(jnp.clip(cols[n * 4 + j] - col * 6, 0, 5) * S, S)
                valid = jnp.logical_and(i < nr, j < nc)
                source = ancestor.at[pl.ds(low, S), pl.ds(left, S)]
                target = first.at[0, j, i] if n == 0 else rest.at[n - 1, j, i]
                inward = pltpu.make_async_copy(source, tiles.at[n, i, j], sems.at[n, i, j])
                outward = pltpu.make_async_copy(tiles.at[n, i, j], target, out_sems.at[n, i, j])
                pl.when(valid)(inward.start)
                moves.append((valid, inward, outward))
    for valid, inward, outward in moves:

        @pl.when(valid)
        def _():
            inward.wait()
            outward.start()

    for valid, inward, outward in moves:
        pl.when(valid)(outward.wait)


def route_kernel(info, fs, pieces, out, table, count):
    x = info[0]
    for i in range(2 * F):
        table[i] = 0
    for i in range(F):
        count[i] = 0
    for p in range(F):
        col = col_of(fs[x, p])
        n = count[col]
        table[col * 2 + jnp.minimum(n, 1)] = p
        count[col] = n + 1
    for i in range(2 * F):
        out[i] = pieces[table[i]]


def product_kernel(steps, base, info, fs, mine, theirs, *refs):
    out, tiles, sems = refs[-3:]
    refs = list(refs[:-3])
    x, c = info[0], info[3]
    r = x * 2 + info[1]
    col = info[2] * 2 + c
    jobs = []
    for n, step in enumerate(steps):
        k = (x + step) & 3
        nr = jnp.minimum(count_if(fs, k, lambda strip: row_of(strip) == r), 4)
        for side, source in enumerate((mine, theirs)):
            nc = count_if(fs, k, lambda strip: col_of(strip) == (col ^ side))
            for j in range(2):
                spot = (n, side, j)
                loop = jnp.where(j < nc, nr, 0)

                def copy(i, n=base + n, j=j, source=source, spot=spot):
                    return pltpu.make_async_copy(
                        source.at[n, j, i], tiles.at[(*spot, i)], sems.at[(*spot, i)]
                    )

                def start(i, carry, copy=copy):
                    copy(i).start()
                    return carry

                lax.fori_loop(0, loop, start, 0)
                jobs.append((n, (c ^ side) * 2 + j, spot, loop, copy))
    out[...] = jnp.zeros_like(out)
    panels = []
    for step in steps:
        panels.append([refs.pop(0) for _ in range(2 if step == 2 else 1)])
    for n, slot, spot, loop, copy in jobs:

        @pl.when(loop > 0)
        def _():
            right = split(
                jnp.concatenate([ref[:, slot] for ref in panels[n]], axis=0).reshape(S, HALF)
            )

            def body(i, carry):
                copy(i).wait()
                value = dot3(split(tiles[(*spot, i)]), right, ((1,), (0,)))
                out[:, n, i] += value.reshape(16, PIECE, HALF)
                return carry

            lax.fori_loop(0, loop, body, 0)


def homes_kernel(info, fs, *refs):
    pieces, out, table, count = refs[:4], refs[4], refs[5], refs[6]
    x = info[0]
    for i in range(8):
        count[i] = 0
    for p in range(F):
        r = row_of(fs[x, p])
        n = count[r]
        table[r * 4 + jnp.minimum(n, 3)] = p
        count[r] = n + 1
    for dx in range(4):
        for h in range(2):
            r = ((x + dx) & 3) * 2 + h
            for i in range(4):

                @pl.when(i < count[r])
                def _():
                    p = table[r * 4 + i]
                    piece = pieces[dx][h, i]
                    out[p] = piece
                    out[F + p] = piece


def strip_kernel(info, fs, pieces, panel, strip, upper, keep, send, tmp):
    h, c = info[1], info[3]
    parts = [pieces[:, ch].reshape(S, HALF) for ch in range(2)]
    value = jnp.concatenate(parts, axis=1)
    strip[...] = -value
    upper[0, 0] = -value
    tmp[...] = dot3(split(panel[0, 0]), split(value), ((0,), (0,)))
    for xx in range(4):
        low = pl.multiple_of((xx * 2 + h) * 64, 64)
        for out, ch in ((keep, c), (send, 1 - c)):
            lanes = pl.multiple_of(ch * HALF, HALF)
            out[:, xx] = tmp[pl.ds(low, 64), pl.ds(lanes, HALF)].reshape(8, 8, HALF)


VMEM = pl.BlockSpec(memory_space=pltpu.VMEM)
ANY = pl.BlockSpec(memory_space=pl.ANY)


def call(kernel, info, fs, args, out_shapes, in_specs=None, out_specs=None, scratch=(), flops=0):
    single = not isinstance(out_shapes, list)
    shapes = [out_shapes] if single else out_shapes
    out_shape = [jax.ShapeDtypeStruct(s, jnp.float32) for s in shapes]
    moved = 4 * sum(functools.reduce(lambda a, b: a * b, s) for s in shapes)
    return pl.pallas_call(
        kernel,
        out_shape=out_shape[0] if single else out_shape,
        grid_spec=pltpu.PrefetchScalarGridSpec(
            num_scalar_prefetch=2,
            grid=(1,),
            in_specs=in_specs or [VMEM] * len(args),
            out_specs=out_specs or (VMEM if single else [VMEM] * len(shapes)),
            scratch_shapes=list(scratch),
        ),
        compiler_params=pltpu.CompilerParams(vmem_limit_bytes=LIMIT),
        cost_estimate=pl.CostEstimate(flops=flops, bytes_accessed=2 * moved, transcendentals=0),
    )(info, fs, *args)


def hop(value, axis, shift):
    size = SIZES[AXES.index(axis)]
    return lax.ppermute(value, axis, [(i, (i + shift) % size) for i in range(size)])


def exchange(value, axes):
    return lax.all_to_all(value, axes, 0, 0, tiled=True)


def gather_x(value):
    half = value.shape[0] // 2
    before = hop(value, "x", 1)
    after = hop(value, "x", -1)
    top = hop(before[:half], "x", 1)
    bottom = hop(after[half:], "x", -1)
    return before, after, top, bottom


def local(ancestor, panels, diag_inverse, fs):
    x, h, c = lax.axis_index("x"), lax.axis_index("h"), lax.axis_index("c")
    info = jnp.stack([x, h, lax.axis_index(PLANE), c]).astype(jnp.int32)
    own_panel = pl.BlockSpec((1, 1, S, W), lambda i, info, fs: (info[0], 0, 0, 0))

    packed = call(pack_kernel, info, fs, [panels], (8, 2, FRONT, HALF), in_specs=[own_panel])
    pieces = exchange(packed.reshape(F, FRONT, HALF), COL)
    routed = call(
        route_kernel, info, fs, [pieces], (2 * F, FRONT, HALF),
        scratch=[pltpu.SMEM((2 * F,), jnp.int32), pltpu.SMEM((F,), jnp.int32)],
    )
    panel = exchange(routed.reshape(8, 4, FRONT, HALF), PLANE)
    first_tiles, rest_tiles = call(
        gather_kernel, info, fs, [ancestor, packed], [(1, 2, 4, S, S), (3, 2, 4, S, S)],
        in_specs=[ANY, ANY], out_specs=[ANY, ANY],
        scratch=[pltpu.VMEM((K, 4, 2, S, S), jnp.float32),
                 pltpu.SMEM((K * 8,), jnp.int32), pltpu.SMEM((K * 4,), jnp.int32),
                 pltpu.SemaphoreType.DMA((K, 4, 2)), pltpu.SemaphoreType.DMA((K, 4, 2))],
    )
    first_pair = [first_tiles, hop(first_tiles, "c", 1)]
    rest_pair = [rest_tiles, hop(rest_tiles, "c", 1)]
    before, after, top, bottom = gather_x(panel)

    def product(steps, base, pair, blocks, behind=()):
        n = len(steps)
        return call(
            functools.partial(product_kernel, steps, base), info, fs,
            [*pair, *blocks, *behind], (16, n, 4, PIECE, HALF),
            in_specs=[ANY] * 2 + [VMEM] * len(blocks) + [ANY] * len(behind),
            scratch=[pltpu.VMEM((n, 2, 2, 4, S, S), jnp.float32),
                     pltpu.SemaphoreType.DMA((n, 2, 2, 4))],
            flops=n * 10**9,
        )

    def total(value):
        value = exchange(value, SHEET)
        value = value.reshape(2, 8, *value.shape[1:]).sum(1)
        return [value[:, n] for n in range(value.shape[1])]

    own_product = product((0,), 0, first_pair, [panel])
    (own,) = total(own_product)
    near_product = product((3, 1), 0, rest_pair, [before, after], [own])
    near = total(near_product)
    far_product = product((2,), 2, rest_pair, [top, bottom], [near_product])
    near, far_product = lax.optimization_barrier((near, far_product))
    (far,) = total(far_product)
    sources = [own, hop(near[0], "x", -1), hop(far, "x", 2), hop(near[1], "x", 1)]
    homes = call(
        homes_kernel, info, fs, sources, (2 * F, PIECE, HALF),
        scratch=[pltpu.SMEM((32,), jnp.int32), pltpu.SMEM((8,), jnp.int32)],
    )
    placed = exchange(homes, ("h", *COL)).reshape(16, 2, PIECE, HALF)
    strip, upper, part, part_send = call(
        strip_kernel, info, fs, [placed, panels],
        [(S, W), (K, 1, S, W), (8, 4, 8, HALF), (8, 4, 8, HALF)], in_specs=[VMEM, own_panel],
        out_specs=[VMEM, own_panel, VMEM, VMEM],
        scratch=[pltpu.VMEM((W, W), jnp.float32)],
    )
    before, after, top, bottom = gather_x(strip)
    part = exchange(part + hop(part_send, "c", 1), PLANE).sum(0)
    part = exchange(part, ("x",))
    part = exchange(jnp.broadcast_to(part[None], (8, *part.shape)), PLANE)
    for value, step, low in ((before, 3, 0), (after, 1, 0), (top, 2, 0), (bottom, 2, S // 2)):
        k = (x + step) & 3
        upper = lax.dynamic_update_slice(upper, value[None, None], (k, 0, low, 0))
    part = part.transpose(1, 0, 2, 3).reshape(K, 64, HALF)
    theirs = hop(part, "c", 1)
    diagonal = diag_inverse + jnp.where(
        c == 0,
        jnp.concatenate([part, theirs], axis=2),
        jnp.concatenate([theirs, part], axis=2),
    )
    return upper, diagonal


def solution(mesh):
    return jax.shard_map(
        local,
        mesh=Mesh(mesh.devices.reshape(SIZES), AXES),
        in_specs=(P(ROW, COL), P(None, COL, None, None), P(None, ROW, None), P()),
        out_specs=(P(None, COL, None, None), P(None, ROW, None)),
        check_vma=False,
    )
```

```python
import functools

import jax
import jax.numpy as jnp
from jax import lax
from jax.experimental import pallas as pl
from jax.experimental.pallas import tpu as pltpu
from jax.sharding import Mesh
from jax.sharding import PartitionSpec as P


AXES = ("x", "h", "l", "z", "c")
SIZES = (4, 2, 2, 4, 2)
ROW, COL, PLANE = ("x", "h"), ("l", "z", "c"), ("l", "z")
SHEET = ("h", *PLANE)
S = 256
W = 512
K = 4
F = 16
HALF = W // 2
FRONT = S // 8
PIECE = S // 16
STEPS = (0, 3, 1, 2)


def col_of(strip):
    return (strip * 43) >> 8


def row_of(strip):
    return col_of(strip) >> 1


def split(value):
    high = value.astype(jnp.bfloat16)
    low = (value - high.astype(jnp.float32)).astype(jnp.bfloat16)
    return high, low


def dot3(left, right, dims):
    (lh, ll), (rh, rl) = left, right
    one = functools.partial(
        lax.dot_general, dimension_numbers=(dims, ((), ())), preferred_element_type=jnp.float32
    )
    return one(lh, rh) + (one(lh, rl) + one(ll, rh))


def pack_kernel(fs, panels, out, panel, sem):
    copy = pltpu.make_async_copy(panels.at[lax.axis_index("x"), 0], panel, sem)
    copy.start()
    copy.wait()
    for ch in range(2):
        out[:, ch] = panel[:, ch * HALF : (ch + 1) * HALF].reshape(8, FRONT, HALF)


def count_if(fs, k, test):
    total = jnp.int32(0)
    for p in range(F):
        total = total + test(fs[k, p]).astype(jnp.int32)
    return total


def gather_kernel(fs, ancestor, after, first, rest, tiles, rows, cols, sems, out_sems):
    r = lax.axis_index("x") * 2 + lax.axis_index("h")
    col = lax.axis_index(PLANE) * 2 + lax.axis_index("c")
    moves = []
    for n, step in enumerate(STEPS):
        k = (lax.axis_index("x") + step) & 3
        nr = jnp.int32(0)
        nc = jnp.int32(0)
        for i in range(8):
            rows[n * 8 + i] = r * 12
        for i in range(4):
            cols[n * 4 + i] = col * 6
        for p in range(F):
            strip = fs[k, p]
            rows[n * 8 + jnp.minimum(nr, 7)] = strip
            cols[n * 4 + jnp.minimum(nc, 3)] = strip
            nr = nr + (row_of(strip) == r).astype(jnp.int32)
            nc = nc + (col_of(strip) == col).astype(jnp.int32)
        for i in range(4):
            low = pl.multiple_of(jnp.clip(rows[n * 8 + i] - r * 12, 0, 11) * S, S)
            for j in range(2):
                left = pl.multiple_of(jnp.clip(cols[n * 4 + j] - col * 6, 0, 5) * S, S)
                valid = jnp.logical_and(i < nr, j < nc)
                source = ancestor.at[pl.ds(low, S), pl.ds(left, S)]
                target = first.at[0, j, i] if n == 0 else rest.at[n - 1, j, i]
                inward = pltpu.make_async_copy(source, tiles.at[n, i, j], sems.at[n, i, j])
                outward = pltpu.make_async_copy(tiles.at[n, i, j], target, out_sems.at[n, i, j])
                pl.when(valid)(inward.start)
                moves.append((valid, inward, outward))
    for valid, inward, outward in moves:

        @pl.when(valid)
        def _():
            inward.wait()
            outward.start()

    for valid, inward, outward in moves:
        pl.when(valid)(outward.wait)


def route_kernel(fs, pieces, out, table, count):
    x = lax.axis_index("x")
    for i in range(2 * F):
        table[i] = 0
    for i in range(F):
        count[i] = 0
    for p in range(F):
        col = col_of(fs[x, p])
        n = count[col]
        table[col * 2 + jnp.minimum(n, 1)] = p
        count[col] = n + 1
    for i in range(2 * F):
        out[i] = pieces[table[i]]


def product_kernel(steps, base, fs, mine, theirs, *refs):
    out, tiles, sems = refs[-3:]
    refs = list(refs[:-3])
    x, c = lax.axis_index("x"), lax.axis_index("c")
    r = x * 2 + lax.axis_index("h")
    col = lax.axis_index(PLANE) * 2 + c
    jobs = []
    for n, step in enumerate(steps):
        k = (x + step) & 3
        nr = jnp.minimum(count_if(fs, k, lambda strip: row_of(strip) == r), 4)
        for side, source in enumerate((mine, theirs)):
            nc = count_if(fs, k, lambda strip: col_of(strip) == (col ^ side))
            for j in range(2):
                spot = (n, side, j)
                loop = jnp.where(j < nc, nr, 0)

                def copy(i, n=base + n, j=j, source=source, spot=spot):
                    return pltpu.make_async_copy(
                        source.at[n, j, i], tiles.at[(*spot, i)], sems.at[(*spot, i)]
                    )

                def start(i, carry, copy=copy):
                    copy(i).start()
                    return carry

                lax.fori_loop(0, loop, start, 0)
                jobs.append((n, (c ^ side) * 2 + j, spot, loop, copy))
    out[...] = jnp.zeros_like(out)
    panels = []
    for step in steps:
        panels.append([refs.pop(0) for _ in range(2 if step == 2 else 1)])
    for n, slot, spot, loop, copy in jobs:

        @pl.when(loop > 0)
        def _():
            right = split(
                jnp.concatenate([ref[:, slot] for ref in panels[n]], axis=0).reshape(S, HALF)
            )

            def body(i, carry):
                copy(i).wait()
                value = dot3(split(tiles[(*spot, i)]), right, ((1,), (0,)))
                out[:, n, i] += value.reshape(16, PIECE, HALF)
                return carry

            lax.fori_loop(0, loop, body, 0)


def homes_kernel(fs, *refs):
    pieces, out, table, count = refs[:4], refs[4], refs[5], refs[6]
    x = lax.axis_index("x")
    for i in range(8):
        count[i] = 0
    for p in range(F):
        r = row_of(fs[x, p])
        n = count[r]
        table[r * 4 + jnp.minimum(n, 3)] = p
        count[r] = n + 1
    for dx in range(4):
        for h in range(2):
            r = ((x + dx) & 3) * 2 + h
            for i in range(4):

                @pl.when(i < count[r])
                def _():
                    p = table[r * 4 + i]
                    piece = pieces[dx][h, i]
                    out[p] = piece
                    out[F + p] = piece


def strip_kernel(fs, pieces, panels, strip, upper, keep, send, tmp, panel, sems):
    x = lax.axis_index("x")
    fetch = pltpu.make_async_copy(panels.at[x, 0], panel, sems.at[0])
    fetch.start()
    h, c = lax.axis_index("h"), lax.axis_index("c")
    parts = [pieces[:, ch].reshape(S, HALF) for ch in range(2)]
    value = jnp.concatenate(parts, axis=1)
    strip[...] = -value
    store = pltpu.make_async_copy(strip, upper.at[x, 0], sems.at[1])
    store.start()
    fetch.wait()
    tmp[...] = dot3(split(panel[...]), split(value), ((0,), (0,)))
    for xx in range(4):
        low = pl.multiple_of((xx * 2 + h) * 64, 64)
        for out, ch in ((keep, c), (send, 1 - c)):
            lanes = pl.multiple_of(ch * HALF, HALF)
            out[xx] = tmp[pl.ds(low, 64), pl.ds(lanes, HALF)].reshape(8, 8, HALF)
    store.wait()


VMEM = pl.BlockSpec(memory_space=pltpu.VMEM)
ANY = pl.BlockSpec(memory_space=pl.ANY)
SMEM = pl.BlockSpec(memory_space=pltpu.SMEM)
HBM = pl.BlockSpec(memory_space=pltpu.HBM)


def call(kernel, fs, args, out_shapes, in_specs=None, out_specs=None, scratch=(), flops=0, mib=8):
    single = not isinstance(out_shapes, list)
    shapes = [out_shapes] if single else out_shapes
    out_shape = [jax.ShapeDtypeStruct(s, jnp.float32) for s in shapes]
    moved = 4 * sum(functools.reduce(lambda a, b: a * b, s) for s in shapes)
    return pl.pallas_call(
        kernel,
        out_shape=out_shape[0] if single else out_shape,
        in_specs=[SMEM, *(in_specs or [VMEM] * len(args))],
        out_specs=out_specs or (VMEM if single else [VMEM] * len(shapes)),
        scratch_shapes=list(scratch),
        compiler_params=pltpu.CompilerParams(vmem_limit_bytes=mib * 1024 * 1024),
        cost_estimate=pl.CostEstimate(flops=flops, bytes_accessed=2 * moved, transcendentals=0),
    )(fs, *args)


def hop(value, axis, shift):
    size = SIZES[AXES.index(axis)]
    return lax.ppermute(value, axis, [(i, (i + shift) % size) for i in range(size)])


def exchange(value, axes):
    return lax.all_to_all(value, axes, 0, 0, tiled=True)


def gather_x(value):
    half = value.shape[0] // 2
    before = hop(value, "x", 1)
    after = hop(value, "x", -1)
    top = hop(before[:half], "x", 1)
    bottom = hop(after[half:], "x", -1)
    return before, after, top, bottom


def local(ancestor, panels, diag_inverse, fs):
    x, c = lax.axis_index("x"), lax.axis_index("c")
    packed = call(
        pack_kernel, fs, [panels], (8, 2, FRONT, HALF), in_specs=[HBM],
        scratch=[pltpu.VMEM((S, W), jnp.float32), pltpu.SemaphoreType.DMA], mib=60,
    )
    pieces = exchange(packed.reshape(F, FRONT, HALF), COL)
    routed = call(
        route_kernel, fs, [pieces], (2 * F, FRONT, HALF),
        scratch=[pltpu.SMEM((2 * F,), jnp.int32), pltpu.SMEM((F,), jnp.int32)],
    )
    panel = exchange(routed.reshape(8, 4, FRONT, HALF), PLANE)
    first_tiles, rest_tiles = call(
        gather_kernel, fs, [ancestor, packed], [(1, 2, 4, S, S), (3, 2, 4, S, S)],
        in_specs=[HBM, ANY], out_specs=[HBM, HBM],
        scratch=[pltpu.VMEM((K, 4, 2, S, S), jnp.float32),
                 pltpu.SMEM((K * 8,), jnp.int32), pltpu.SMEM((K * 4,), jnp.int32),
                 pltpu.SemaphoreType.DMA((K, 4, 2)), pltpu.SemaphoreType.DMA((K, 4, 2))],
        mib=60,
    )
    first_pair = [first_tiles, hop(first_tiles, "c", 1)]
    rest_pair = [rest_tiles, hop(rest_tiles, "c", 1)]
    before, after, top, bottom = gather_x(panel)

    def product(steps, base, pair, blocks, behind=()):
        n = len(steps)
        return call(
            functools.partial(product_kernel, steps, base), fs,
            [*pair, *blocks, *behind], (16, n, 4, PIECE, HALF),
            in_specs=[HBM] * 2 + [VMEM] * len(blocks) + [ANY] * len(behind),
            scratch=[pltpu.VMEM((n, 2, 2, 4, S, S), jnp.float32),
                     pltpu.SemaphoreType.DMA((n, 2, 2, 4))],
            flops=n * 10**9, mib=8 * n + 6,
        )

    def total(value):
        value = exchange(value, SHEET)
        value = value.reshape(2, 8, *value.shape[1:])
        return [value[:, :, n].sum(1) for n in range(value.shape[2])]

    own_product = product((0,), 0, first_pair, [panel])
    (own,) = total(own_product)
    near_product = product((3, 1), 0, rest_pair, [before, after], [own])
    near = total(near_product)
    far_product = product((2,), 2, rest_pair, [top, bottom], [near_product])
    near, far_product = lax.optimization_barrier((near, far_product))
    (far,) = total(far_product)
    sources = [own, hop(near[0], "x", -1), hop(far, "x", 2), hop(near[1], "x", 1)]
    homes = call(
        homes_kernel, fs, sources, (2 * F, PIECE, HALF),
        scratch=[pltpu.SMEM((32,), jnp.int32), pltpu.SMEM((8,), jnp.int32)],
    )
    placed = exchange(homes, ("h", *COL)).reshape(16, 2, PIECE, HALF)
    strip, upper, part, part_send = call(
        strip_kernel, fs, [placed, panels],
        [(S, W), (K, 1, S, W), (4, 8, 8, HALF), (4, 8, 8, HALF)], in_specs=[VMEM, HBM],
        out_specs=[VMEM, HBM, VMEM, VMEM],
        scratch=[pltpu.VMEM((W, W), jnp.float32), pltpu.VMEM((S, W), jnp.float32),
                 pltpu.SemaphoreType.DMA((2,))],
    )
    before, after, top, bottom = gather_x(strip)
    part = (part + hop(part_send, "c", 1)).reshape(32, 8, HALF)
    part = exchange(part, ("x", *PLANE))
    part = part.reshape(4, 8, 8, HALF).sum(1)
    part = exchange(jnp.broadcast_to(part[None], (8, *part.shape)), PLANE)
    for value, step, low in ((before, 3, 0), (after, 1, 0), (top, 2, 0), (bottom, 2, S // 2)):
        k = (x + step) & 3
        upper = lax.dynamic_update_slice(upper, value[None, None], (k, 0, low, 0))
    part = part.transpose(1, 0, 2, 3).reshape(K, 64, HALF)
    theirs = hop(part, "c", 1)
    diagonal = diag_inverse + jnp.where(
        c == 0,
        jnp.concatenate([part, theirs], axis=2),
        jnp.concatenate([theirs, part], axis=2),
    )
    return upper, diagonal


def solution(mesh):
    return jax.shard_map(
        local,
        mesh=Mesh(mesh.devices.reshape(SIZES), AXES),
        in_specs=(P(ROW, COL), P(None, COL, None, None), P(None, ROW, None), P()),
        out_specs=(P(None, COL, None, None), P(None, ROW, None)),
        check_vma=False,
    )
```

```python
import functools

import jax
import jax.numpy as jnp
from jax import lax
from jax.experimental import pallas as pl
from jax.experimental.pallas import tpu as pltpu
from jax.sharding import Mesh
from jax.sharding import PartitionSpec as P


AXES = ("x", "h", "l", "z", "c")
SIZES = (4, 2, 2, 4, 2)
ROW, COL, PLANE = ("x", "h"), ("l", "z", "c"), ("l", "z")
SHEET = ("h", *PLANE)
S = 256
W = 512
K = 4
F = 16
HALF = W // 2
FRONT = S // 8
PIECE = S // 16
STEPS = (0, 3, 1, 2)


def col_of(strip):
    return (strip * 43) >> 8


def row_of(strip):
    return col_of(strip) >> 1


def split(value):
    high = value.astype(jnp.bfloat16)
    low = (value - high.astype(jnp.float32)).astype(jnp.bfloat16)
    return high, low


def dot3(left, right, dims):
    (lh, ll), (rh, rl) = left, right
    one = functools.partial(
        lax.dot_general, dimension_numbers=(dims, ((), ())), preferred_element_type=jnp.float32
    )
    return one(lh, rh) + (one(lh, rl) + one(ll, rh))


def pack_kernel(fs, panels, out, panel, sem):
    copy = pltpu.make_async_copy(panels.at[lax.axis_index("x"), 0], panel, sem)
    copy.start()
    copy.wait()
    for ch in range(2):
        out[:, ch] = panel[:, ch * HALF : (ch + 1) * HALF].reshape(8, FRONT, HALF)


def count_if(fs, k, test):
    total = jnp.int32(0)
    for p in range(F):
        total = total + test(fs[k, p]).astype(jnp.int32)
    return total


def gather_kernel(fs, ancestor, after, first, rest, tiles, rows, cols, sems, out_sems):
    r = lax.axis_index("x") * 2 + lax.axis_index("h")
    col = lax.axis_index(PLANE) * 2 + lax.axis_index("c")
    moves = []
    for n, step in enumerate(STEPS):
        k = (lax.axis_index("x") + step) & 3
        nr = jnp.int32(0)
        nc = jnp.int32(0)
        for i in range(8):
            rows[n * 8 + i] = r * 12
        for i in range(4):
            cols[n * 4 + i] = col * 6
        for p in range(F):
            strip = fs[k, p]
            rows[n * 8 + jnp.minimum(nr, 7)] = strip
            cols[n * 4 + jnp.minimum(nc, 3)] = strip
            nr = nr + (row_of(strip) == r).astype(jnp.int32)
            nc = nc + (col_of(strip) == col).astype(jnp.int32)
        for i in range(4):
            low = pl.multiple_of(jnp.clip(rows[n * 8 + i] - r * 12, 0, 11) * S, S)
            for j in range(2):
                left = pl.multiple_of(jnp.clip(cols[n * 4 + j] - col * 6, 0, 5) * S, S)
                valid = jnp.logical_and(i < nr, j < nc)
                source = ancestor.at[pl.ds(low, S), pl.ds(left, S)]
                target = first.at[0, j, i] if n == 0 else rest.at[n - 1, j, i]
                inward = pltpu.make_async_copy(source, tiles.at[n, i, j], sems.at[n, i, j])
                outward = pltpu.make_async_copy(tiles.at[n, i, j], target, out_sems.at[n, i, j])
                pl.when(valid)(inward.start)
                moves.append((valid, inward, outward))
    for valid, inward, outward in moves:

        @pl.when(valid)
        def _():
            inward.wait()
            outward.start()

    for valid, inward, outward in moves:
        pl.when(valid)(outward.wait)


def route_kernel(fs, pieces, out, table, count):
    x = lax.axis_index("x")
    for i in range(2 * F):
        table[i] = 0
    for i in range(F):
        count[i] = 0
    for p in range(F):
        col = col_of(fs[x, p])
        n = count[col]
        table[col * 2 + jnp.minimum(n, 1)] = p
        count[col] = n + 1
    for i in range(2 * F):
        out[i] = pieces[table[i]]


def product_kernel(steps, base, fs, mine, theirs, *refs):
    out, tiles, sems = refs[-3:]
    refs = list(refs[:-3])
    x, c = lax.axis_index("x"), lax.axis_index("c")
    r = x * 2 + lax.axis_index("h")
    col = lax.axis_index(PLANE) * 2 + c
    jobs = []
    for n, step in enumerate(steps):
        k = (x + step) & 3
        nr = jnp.minimum(count_if(fs, k, lambda strip: row_of(strip) == r), 4)
        for side, source in enumerate((mine, theirs)):
            nc = count_if(fs, k, lambda strip: col_of(strip) == (col ^ side))
            for j in range(2):
                spot = (n, side, j)
                loop = jnp.where(j < nc, nr, 0)

                def copy(i, n=base + n, j=j, source=source, spot=spot):
                    return pltpu.make_async_copy(
                        source.at[n, j, i], tiles.at[(*spot, i)], sems.at[(*spot, i)]
                    )

                def start(i, carry, copy=copy):
                    copy(i).start()
                    return carry

                lax.fori_loop(0, loop, start, 0)
                jobs.append((n, (c ^ side) * 2 + j, spot, loop, copy))
    out[...] = jnp.zeros_like(out)
    panels = []
    for step in steps:
        panels.append([refs.pop(0) for _ in range(2 if step == 2 else 1)])
    for n, slot, spot, loop, copy in jobs:

        @pl.when(loop > 0)
        def _():
            right = split(
                jnp.concatenate([ref[:, slot] for ref in panels[n]], axis=0).reshape(S, HALF)
            )

            def body(i, carry):
                copy(i).wait()
                value = dot3(split(tiles[(*spot, i)]), right, ((1,), (0,)))
                if out.shape[0] == 8:
                    out[:, n, i] += value.reshape(8, FRONT, HALF)
                else:
                    value = value.reshape(8, 2, PIECE, HALF)
                    for h in range(2):
                        out[h * 8 : h * 8 + 8, n, i] += value[:, h]
                return carry

            lax.fori_loop(0, loop, body, 0)


def homes_kernel(fs, *refs):
    own, arrived, far, out, table, count = refs
    pieces = [own, *(arrived.at[n] for n in range(5))]
    x, h = lax.axis_index("x"), lax.axis_index("h")
    for i in range(8):
        count[i] = 0
    for p in range(F):
        r = row_of(fs[x, p])
        n = count[r]
        table[r * 4 + jnp.minimum(n, 3)] = p
        count[r] = n + 1
    sources = [(((x + 2) & 3) * 2 + hs, far.at[hs]) for hs in range(2)]
    for n, dx in enumerate((0, 1, 3)):
        for dh in range(2):
            sources.append((((x + dx) & 3) * 2 + (h ^ dh), pieces[n * 2 + dh]))
    for r, source in sources:
        for i in range(4):

            @pl.when(i < count[r])
            def _():
                p = table[r * 4 + i]
                piece = source[i]
                out[p] = piece
                out[F + p] = piece


def strip_kernel(fs, pieces, panels, strip, upper, keep, send, tmp, panel, sems):
    x = lax.axis_index("x")
    fetch = pltpu.make_async_copy(panels.at[x, 0], panel, sems.at[0])
    fetch.start()
    h, c = lax.axis_index("h"), lax.axis_index("c")
    parts = [
        jnp.stack([pieces[0, :, ch], pieces[1, :, ch]], axis=1).reshape(S, HALF) for ch in range(2)
    ]
    value = jnp.concatenate(parts, axis=1)
    strip[...] = -value
    store = pltpu.make_async_copy(strip, upper.at[x, 0], sems.at[1])
    store.start()
    fetch.wait()
    tmp[...] = dot3(split(panel[...]), split(value), ((0,), (0,)))
    for xx in range(4):
        low = pl.multiple_of((xx * 2 + h) * 64, 64)
        for out, ch in ((keep, c), (send, 1 - c)):
            lanes = pl.multiple_of(ch * HALF, HALF)
            out[xx] = tmp[pl.ds(low, 64), pl.ds(lanes, HALF)].reshape(8, 8, HALF)
    store.wait()


VMEM = pl.BlockSpec(memory_space=pltpu.VMEM)
ANY = pl.BlockSpec(memory_space=pl.ANY)
SMEM = pl.BlockSpec(memory_space=pltpu.SMEM)
HBM = pl.BlockSpec(memory_space=pltpu.HBM)


def call(kernel, fs, args, out_shapes, in_specs=None, out_specs=None, scratch=(), flops=0, mib=8):
    single = not isinstance(out_shapes, list)
    shapes = [out_shapes] if single else out_shapes
    out_shape = [jax.ShapeDtypeStruct(s, jnp.float32) for s in shapes]
    moved = 4 * sum(functools.reduce(lambda a, b: a * b, s) for s in shapes)
    return pl.pallas_call(
        kernel,
        out_shape=out_shape[0] if single else out_shape,
        in_specs=[SMEM, *(in_specs or [VMEM] * len(args))],
        out_specs=out_specs or (VMEM if single else [VMEM] * len(shapes)),
        scratch_shapes=list(scratch),
        compiler_params=pltpu.CompilerParams(vmem_limit_bytes=mib * 1024 * 1024),
        cost_estimate=pl.CostEstimate(flops=flops, bytes_accessed=2 * moved, transcendentals=0),
    )(fs, *args)


def hop(value, axis, shift):
    size = SIZES[AXES.index(axis)]
    return lax.ppermute(value, axis, [(i, (i + shift) % size) for i in range(size)])


def exchange(value, axes):
    return lax.all_to_all(value, axes, 0, 0, tiled=True)


def row_hop(value, dx, dh):
    pairs = [(x * 2 + h, (x + dx) % 4 * 2 + (h ^ dh)) for x in range(4) for h in range(2)]
    return lax.ppermute(value, ROW, pairs)


def gather_x(value):
    half = value.shape[0] // 2
    before = hop(value, "x", 1)
    after = hop(value, "x", -1)
    top = hop(before[:half], "x", 1)
    bottom = hop(after[half:], "x", -1)
    return before, after, top, bottom


def local(ancestor, panels, diag_inverse, fs):
    x, h, c = lax.axis_index("x"), lax.axis_index("h"), lax.axis_index("c")
    packed = call(
        pack_kernel, fs, [panels], (8, 2, FRONT, HALF), in_specs=[HBM],
        scratch=[pltpu.VMEM((S, W), jnp.float32), pltpu.SemaphoreType.DMA], mib=60,
    )
    pieces = exchange(packed.reshape(F, FRONT, HALF), COL)
    routed = call(
        route_kernel, fs, [pieces], (2 * F, FRONT, HALF),
        scratch=[pltpu.SMEM((2 * F,), jnp.int32), pltpu.SMEM((F,), jnp.int32)],
    )
    panel = exchange(routed.reshape(8, 4, FRONT, HALF), PLANE)
    first_tiles, rest_tiles = call(
        gather_kernel, fs, [ancestor, packed], [(1, 2, 4, S, S), (3, 2, 4, S, S)],
        in_specs=[HBM, ANY], out_specs=[HBM, HBM],
        scratch=[pltpu.VMEM((K, 4, 2, S, S), jnp.float32),
                 pltpu.SMEM((K * 8,), jnp.int32), pltpu.SMEM((K * 4,), jnp.int32),
                 pltpu.SemaphoreType.DMA((K, 4, 2)), pltpu.SemaphoreType.DMA((K, 4, 2))],
        mib=60,
    )
    first_pair = [first_tiles, hop(first_tiles, "c", 1)]
    rest_pair = [rest_tiles, hop(rest_tiles, "c", 1)]
    before, after, top, bottom = gather_x(panel)

    def product(steps, base, pair, blocks, behind=()):
        n = len(steps)
        return call(
            functools.partial(product_kernel, steps, base), fs,
            [*pair, *blocks, *behind],
            (16, n, 4, PIECE, HALF) if steps == (2,) else (8, n, 4, FRONT, HALF),
            in_specs=[HBM] * 2 + [VMEM] * len(blocks) + [ANY] * len(behind),
            scratch=[pltpu.VMEM((n, 2, 2, 4, S, S), jnp.float32),
                     pltpu.SemaphoreType.DMA((n, 2, 2, 4))],
            flops=n * 10**9, mib=14 if n == 1 and base == 0 else 50,
        )

    def halves(value):
        value = exchange(value, PLANE).sum(0).reshape(-1, 4, 2, PIECE, HALF)
        return [
            [lax.dynamic_index_in_dim(part, side, 1, keepdims=False) for side in (h, 1 - h)]
            for part in value
        ]

    own_product = product((0,), 0, first_pair, [panel])
    ((own, own_send),) = halves(own_product)
    near_product = product((3, 1), 0, rest_pair, [before, after], [own])
    near = halves(near_product)
    far_product = product((2,), 2, rest_pair, [top, bottom], [near_product])
    near, far_product = lax.optimization_barrier((near, far_product))
    far = exchange(far_product, SHEET)
    far = far.reshape(2, 8, 4, PIECE, HALF).sum(1)
    sources = [row_hop(own_send, 0, 1)]
    for (keep, send), dx in zip(near, (-1, 1), strict=True):
        sources += [row_hop(keep, dx, 0), row_hop(send, dx, 1)]
    sources = [own, jnp.stack(sources), hop(far, "x", 2)]
    homes = call(
        homes_kernel, fs, sources, (2 * F, PIECE, HALF),
        scratch=[pltpu.SMEM((32,), jnp.int32), pltpu.SMEM((8,), jnp.int32)],
    )
    placed = exchange(homes, ("h", *COL)).reshape(2, 8, 2, PIECE, HALF)
    strip, upper, part, part_send = call(
        strip_kernel, fs, [placed, panels],
        [(S, W), (K, 1, S, W), (4, 8, 8, HALF), (4, 8, 8, HALF)], in_specs=[VMEM, HBM],
        out_specs=[VMEM, HBM, VMEM, VMEM],
        scratch=[pltpu.VMEM((W, W), jnp.float32), pltpu.VMEM((S, W), jnp.float32),
                 pltpu.SemaphoreType.DMA((2,))],
    )
    before, after, top, bottom = gather_x(strip)
    part = (part + hop(part_send, "c", 1)).reshape(32, 8, HALF)
    part = exchange(part, ("x", *PLANE))
    part = part.reshape(4, 8, 8, HALF).sum(1)
    part = exchange(jnp.broadcast_to(part[None], (8, *part.shape)), PLANE)
    for value, step, low in ((before, 3, 0), (after, 1, 0), (top, 2, 0), (bottom, 2, S // 2)):
        k = (x + step) & 3
        upper = lax.dynamic_update_slice(upper, value[None, None], (k, 0, low, 0))
    part = part.transpose(1, 0, 2, 3).reshape(K, 64, HALF)
    theirs = hop(part, "c", 1)
    diagonal = diag_inverse + jnp.where(
        c == 0,
        jnp.concatenate([part, theirs], axis=2),
        jnp.concatenate([theirs, part], axis=2),
    )
    return upper, diagonal


def solution(mesh):
    return jax.shard_map(
        local,
        mesh=Mesh(mesh.devices.reshape(SIZES), AXES),
        in_specs=(P(ROW, COL), P(None, COL, None, None), P(None, ROW, None), P()),
        out_specs=(P(None, COL, None, None), P(None, ROW, None)),
        check_vma=False,
    )
```

```python
import functools

import jax
import jax.numpy as jnp
from jax import lax
from jax.experimental import pallas as pl
from jax.experimental.pallas import tpu as pltpu
from jax.sharding import Mesh
from jax.sharding import PartitionSpec as P


AXES = ("x", "h", "l", "z", "c")
SIZES = (4, 2, 2, 4, 2)
ROW, COL, PLANE = ("x", "h"), ("l", "z", "c"), ("l", "z")
SHEET = ("h", *PLANE)
S = 256
W = 512
K = 4
F = 16
HALF = W // 2
FRONT = S // 8
PIECE = S // 16
STEPS = (0, 3, 1, 2)


def col_of(strip):
    return (strip * 43) >> 8


def row_of(strip):
    return col_of(strip) >> 1


def split(value):
    high = value.astype(jnp.bfloat16)
    low = (value - high.astype(jnp.float32)).astype(jnp.bfloat16)
    return high, low


def dot3(left, right, dims):
    (lh, ll), (rh, rl) = left, right
    one = functools.partial(
        lax.dot_general, dimension_numbers=(dims, ((), ())), preferred_element_type=jnp.float32
    )
    return one(lh, rh) + (one(lh, rl) + one(ll, rh))


def pack_kernel(fs, panels, out, panel, sem):
    copy = pltpu.make_async_copy(panels.at[lax.axis_index("x"), 0], panel, sem)
    copy.start()
    copy.wait()
    for ch in range(2):
        out[:, ch] = panel[:, ch * HALF : (ch + 1) * HALF].reshape(8, FRONT, HALF)


def count_if(fs, k, test):
    total = jnp.int32(0)
    for p in range(F):
        total = total + test(fs[k, p]).astype(jnp.int32)
    return total


def gather_kernel(fs, ancestor, after, first, rest, tiles, rows, cols, sems, out_sems):
    r = lax.axis_index("x") * 2 + lax.axis_index("h")
    col = lax.axis_index(PLANE) * 2 + lax.axis_index("c")
    moves = []
    for n, step in enumerate(STEPS):
        k = (lax.axis_index("x") + step) & 3
        nr = jnp.int32(0)
        nc = jnp.int32(0)
        for i in range(8):
            rows[n * 8 + i] = r * 12
        for i in range(4):
            cols[n * 4 + i] = col * 6
        for p in range(F):
            strip = fs[k, p]
            rows[n * 8 + jnp.minimum(nr, 7)] = strip
            cols[n * 4 + jnp.minimum(nc, 3)] = strip
            nr = nr + (row_of(strip) == r).astype(jnp.int32)
            nc = nc + (col_of(strip) == col).astype(jnp.int32)
        for i in range(4):
            low = pl.multiple_of(jnp.clip(rows[n * 8 + i] - r * 12, 0, 11) * S, S)
            for j in range(2):
                left = pl.multiple_of(jnp.clip(cols[n * 4 + j] - col * 6, 0, 5) * S, S)
                valid = jnp.logical_and(i < nr, j < nc)
                source = ancestor.at[pl.ds(low, S), pl.ds(left, S)]
                target = first.at[0, j, i] if n == 0 else rest.at[n - 1, j, i]
                inward = pltpu.make_async_copy(source, tiles.at[n, i, j], sems.at[n, i, j])
                outward = pltpu.make_async_copy(tiles.at[n, i, j], target, out_sems.at[n, i, j])
                pl.when(valid)(inward.start)
                moves.append((valid, inward, outward))
    for valid, inward, outward in moves:

        @pl.when(valid)
        def _():
            inward.wait()
            outward.start()

    for valid, inward, outward in moves:
        pl.when(valid)(outward.wait)


def route_kernel(fs, pieces, out, table, count):
    x = lax.axis_index("x")
    for i in range(2 * F):
        table[i] = 0
    for i in range(F):
        count[i] = 0
    for p in range(F):
        col = col_of(fs[x, p])
        n = count[col]
        table[col * 2 + jnp.minimum(n, 1)] = p
        count[col] = n + 1
    for i in range(2 * F):
        out[i] = pieces[table[i]]


def product_kernel(steps, base, fs, mine, theirs, *refs):
    out, tiles, sems = refs[-3:]
    refs = list(refs[:-3])
    x, c = lax.axis_index("x"), lax.axis_index("c")
    r = x * 2 + lax.axis_index("h")
    col = lax.axis_index(PLANE) * 2 + c
    jobs = []
    for n, step in enumerate(steps):
        k = (x + step) & 3
        nr = jnp.minimum(count_if(fs, k, lambda strip: row_of(strip) == r), 4)
        for side, source in enumerate((mine, theirs)):
            nc = count_if(fs, k, lambda strip: col_of(strip) == (col ^ side))
            for j in range(2):
                spot = (n, side, j)
                loop = jnp.where(j < nc, nr, 0)

                def copy(i, n=base + n, j=j, source=source, spot=spot):
                    return pltpu.make_async_copy(
                        source.at[n, j, i], tiles.at[(*spot, i)], sems.at[(*spot, i)]
                    )

                def start(i, carry, copy=copy):
                    copy(i).start()
                    return carry

                lax.fori_loop(0, loop, start, 0)
                jobs.append((n, (c ^ side) * 2 + j, spot, loop, copy))
    out[...] = jnp.zeros_like(out)
    panels = []
    for step in steps:
        panels.append([refs.pop(0) for _ in range(2 if step == 2 else 1)])
    for n, slot, spot, loop, copy in jobs:

        @pl.when(loop > 0)
        def _():
            right = split(
                jnp.concatenate([ref[:, slot] for ref in panels[n]], axis=0).reshape(S, HALF)
            )

            def body(i, carry):
                copy(i).wait()
                value = dot3(split(tiles[(*spot, i)]), right, ((1,), (0,)))
                out[:, n, i] += value.reshape(16, PIECE, HALF)
                return carry

            lax.fori_loop(0, loop, body, 0)


def homes_kernel(fs, *refs):
    pieces, out, table, count = refs[:4], refs[4], refs[5], refs[6]
    x = lax.axis_index("x")
    for i in range(8):
        count[i] = 0
    for p in range(F):
        r = row_of(fs[x, p])
        n = count[r]
        table[r * 4 + jnp.minimum(n, 3)] = p
        count[r] = n + 1
    for dx in range(4):
        for h in range(2):
            r = ((x + dx) & 3) * 2 + h
            for i in range(4):

                @pl.when(i < count[r])
                def _():
                    p = table[r * 4 + i]
                    piece = pieces[dx][h, i]
                    out[p] = piece
                    out[F + p] = piece


def strip_kernel(fs, pieces, panels, strip, upper, keep, send, tmp, panel, sems):
    x = lax.axis_index("x")
    fetch = pltpu.make_async_copy(panels.at[x, 0], panel, sems.at[0])
    fetch.start()
    h, c = lax.axis_index("h"), lax.axis_index("c")
    parts = [pieces[:, ch].reshape(S, HALF) for ch in range(2)]
    value = jnp.concatenate(parts, axis=1)
    strip[...] = -value
    store = pltpu.make_async_copy(strip, upper.at[x, 0], sems.at[1])
    store.start()
    fetch.wait()
    tmp[...] = dot3(split(panel[...]), split(value), ((0,), (0,)))
    for xx in range(4):
        low = pl.multiple_of((xx * 2 + h) * 64, 64)
        for out, ch in ((keep, c), (send, 1 - c)):
            lanes = pl.multiple_of(ch * HALF, HALF)
            out[xx] = tmp[pl.ds(low, 64), pl.ds(lanes, HALF)].reshape(8, 8, HALF)
    store.wait()


VMEM = pl.BlockSpec(memory_space=pltpu.VMEM)
ANY = pl.BlockSpec(memory_space=pl.ANY)
SMEM = pl.BlockSpec(memory_space=pltpu.SMEM)
HBM = pl.BlockSpec(memory_space=pltpu.HBM)


def call(kernel, fs, args, out_shapes, in_specs=None, out_specs=None, scratch=(), flops=0, mib=8):
    single = not isinstance(out_shapes, list)
    shapes = [out_shapes] if single else out_shapes
    out_shape = [jax.ShapeDtypeStruct(s, jnp.float32) for s in shapes]
    moved = 4 * sum(functools.reduce(lambda a, b: a * b, s) for s in shapes)
    return pl.pallas_call(
        kernel,
        out_shape=out_shape[0] if single else out_shape,
        in_specs=[SMEM, *(in_specs or [VMEM] * len(args))],
        out_specs=out_specs or (VMEM if single else [VMEM] * len(shapes)),
        scratch_shapes=list(scratch),
        compiler_params=pltpu.CompilerParams(vmem_limit_bytes=mib * 1024 * 1024),
        cost_estimate=pl.CostEstimate(flops=flops, bytes_accessed=2 * moved, transcendentals=0),
    )(fs, *args)


def hop(value, axis, shift):
    size = SIZES[AXES.index(axis)]
    return lax.ppermute(value, axis, [(i, (i + shift) % size) for i in range(size)])


def exchange(value, axes):
    return lax.all_to_all(value, axes, 0, 0, tiled=True)


def gather_x(value):
    half = value.shape[0] // 2
    before = hop(value, "x", 1)
    after = hop(value, "x", -1)
    top = hop(before[:half], "x", 1)
    bottom = hop(after[half:], "x", -1)
    return before, after, top, bottom


def local(ancestor, panels, diag_inverse, fs):
    x, c = lax.axis_index("x"), lax.axis_index("c")
    packed = call(
        pack_kernel, fs, [panels], (8, 2, FRONT, HALF), in_specs=[HBM],
        scratch=[pltpu.VMEM((S, W), jnp.float32), pltpu.SemaphoreType.DMA], mib=60,
    )
    pieces = exchange(packed.reshape(F, FRONT, HALF), COL)
    routed = call(
        route_kernel, fs, [pieces], (2 * F, FRONT, HALF),
        scratch=[pltpu.SMEM((2 * F,), jnp.int32), pltpu.SMEM((F,), jnp.int32)],
    )
    panel = exchange(routed.reshape(8, 4, FRONT, HALF), PLANE)
    first_tiles, rest_tiles = call(
        gather_kernel, fs, [ancestor, packed], [(1, 2, 4, S, S), (3, 2, 4, S, S)],
        in_specs=[HBM, ANY], out_specs=[HBM, HBM],
        scratch=[pltpu.VMEM((K, 4, 2, S, S), jnp.float32),
                 pltpu.SMEM((K * 8,), jnp.int32), pltpu.SMEM((K * 4,), jnp.int32),
                 pltpu.SemaphoreType.DMA((K, 4, 2)), pltpu.SemaphoreType.DMA((K, 4, 2))],
        mib=60,
    )
    first_pair = [first_tiles, hop(first_tiles, "c", 1)]
    rest_pair = [rest_tiles, hop(rest_tiles, "c", 1)]
    before, after, top, bottom = gather_x(panel)

    def product(steps, base, pair, blocks, behind=()):
        n = len(steps)
        return call(
            functools.partial(product_kernel, steps, base), fs,
            [*pair, *blocks, *behind], (16, n, 4, PIECE, HALF),
            in_specs=[HBM] * 2 + [VMEM] * len(blocks) + [ANY] * len(behind),
            scratch=[pltpu.VMEM((n, 2, 2, 4, S, S), jnp.float32),
                     pltpu.SemaphoreType.DMA((n, 2, 2, 4))],
            flops=n * 10**9, mib=14 if n == 1 and base == 0 else 50,
        )

    def total(value):
        value = exchange(value, SHEET)
        value = value.reshape(2, 8, *value.shape[1:])
        return [value[:, :, n].sum(1) for n in range(value.shape[2])]

    own_product = product((0,), 0, first_pair, [panel])
    (own,) = total(own_product)
    near_product = product((3, 1), 0, rest_pair, [before, after], [own])
    near = total(near_product)
    far_product = product((2,), 2, rest_pair, [top, bottom], [near_product])
    near, far_product = lax.optimization_barrier((near, far_product))
    (far,) = total(far_product)
    sources = [own, hop(near[0], "x", -1), hop(far, "x", 2), hop(near[1], "x", 1)]
    homes = call(
        homes_kernel, fs, sources, (2 * F, PIECE, HALF),
        scratch=[pltpu.SMEM((32,), jnp.int32), pltpu.SMEM((8,), jnp.int32)],
    )
    placed = exchange(homes, ("h", *COL)).reshape(16, 2, PIECE, HALF)
    strip, upper, part, part_send = call(
        strip_kernel, fs, [placed, panels],
        [(S, W), (K, 1, S, W), (4, 8, 8, HALF), (4, 8, 8, HALF)], in_specs=[VMEM, HBM],
        out_specs=[VMEM, HBM, VMEM, VMEM],
        scratch=[pltpu.VMEM((W, W), jnp.float32), pltpu.VMEM((S, W), jnp.float32),
                 pltpu.SemaphoreType.DMA((2,))],
    )
    before, after, top, bottom = gather_x(strip)
    part_other = hop(part_send, "c", 1)
    part = (part + part_other).reshape(32, 8, HALF)
    part = exchange(part, ("x", *PLANE))
    part = part.reshape(4, 8, 8, HALF).sum(1)
    part = exchange(jnp.broadcast_to(part[None], (8, *part.shape)), PLANE)
    for value, step, low in ((before, 3, 0), (after, 1, 0), (top, 2, 0), (bottom, 2, S // 2)):
        k = (x + step) & 3
        upper = lax.dynamic_update_slice(upper, value[None, None], (k, 0, low, 0))
    part = part.transpose(1, 0, 2, 3).reshape(K, 64, HALF)
    theirs = hop(part, "c", 1)
    diagonal = diag_inverse + jnp.where(
        c == 0,
        jnp.concatenate([part, theirs], axis=2),
        jnp.concatenate([theirs, part], axis=2),
    )
    return upper, diagonal


def solution(mesh):
    return jax.shard_map(
        local,
        mesh=Mesh(mesh.devices.reshape(SIZES), AXES),
        in_specs=(P(ROW, COL), P(None, COL, None, None), P(None, ROW, None), P()),
        out_specs=(P(None, COL, None, None), P(None, ROW, None)),
        check_vma=False,
    )
```
